32 devices in a mesh: member: 16 (over z, y, x), tensor: 2 (over core).
Axes of the slice: x: 2, y: 2, z: 4, core: 2. Of those that a mesh axis runs over, the one named last changes fastest.
Arguments:
- tokens: bfloat16 [768, 5120], P('member', 'tensor'), may hold values from -6 to 6
- up_weight: bfloat16 [5120, 27648], P('tensor', 'member'), may hold values from -0.078125 to 0.078125
- left_factors: bfloat16 [192, 5120], P('member', 'tensor'), may hold values from -6 to 6
- right_factors: bfloat16 [192, 27648], P('tensor', 'member'), may hold values from -6 to 6
- fitness: float32 [48], replicated, may hold values from -0.6 to 0.6
Outputs:
- hidden: bfloat16 [768, 27648], P('tensor', 'member')
- gradient: bfloat16 [5120, 27648], P('tensor', 'member')
The draws below stay inside these ranges and needn't reach their ends.
All inputs are finite; a program needn't handle non-finite values.
Results may differ from the reference program's by a relative error of at most 0.014.
Values may be sent and summed in bfloat16 or wider, within the bound.
A program may use at most 64 MiB of HBM per device.

```python
import jax
import jax.numpy as jnp

D = 5120
FFN_HIDDEN = 27648
RANK = 4
MEMBER_TOKENS = 16
POPULATION_SIZE = 48
TOKEN_TOTAL = 768
N_TENSOR = 2


def shard_levels(key, dims, cuts, least, high):
    loudness = 1.0
    for dim, shards_of in cuts:
        heights = jax.random.uniform(jax.random.fold_in(jax.random.fold_in(key, 6), dim), (shards_of,), jnp.float32, least / len(cuts), high / len(cuts))
        loudness = loudness * jnp.repeat(jnp.exp(heights), dims[dim] // shards_of).reshape((-1,) + (1,) * (len(dims) - 1 - dim))
    return loudness


def gaussian(own_key, dims, width, limit, pieces=(), held_as=jnp.bfloat16):
    drawn = width * jax.random.normal(own_key, dims, jnp.float32)
    if pieces:
        drawn = drawn * shard_levels(own_key, dims, pieces, -0.22, 0.18)
    return jnp.clip(drawn, -limit, limit).astype(held_as)


def setup_inputs(seed: int = 0) -> dict:
    key_of = jax.random.split(jax.random.key(seed), 6)
    return {
        "tokens": gaussian(key_of[0], (TOKEN_TOTAL, D), 1.0, 6.0, ((0, 16), (1, 2))),
        "up_weight": gaussian(key_of[1], (D, FFN_HIDDEN), D ** -0.5, 0.078125, ((0, 2), (1, 16))),
        "left_factors": gaussian(key_of[2], (POPULATION_SIZE * RANK, D), 1.0, 6.0, ((0, 16), (1, 2))),
        "right_factors": gaussian(key_of[3], (POPULATION_SIZE * RANK, FFN_HIDDEN), 1.0, 6.0, ((0, 2), (1, 16))),
        "fitness": gaussian(key_of[4], (POPULATION_SIZE,), 0.1, 0.6, (), jnp.float32),
    }


def reference(tokens, up_weight, left_factors, right_factors, fitness):
    noise_scale = 0.25 * D ** -0.5
    mixing = noise_scale * RANK ** -0.5
    block_span_width = D // N_TENSOR
    right_factor_wide = right_factors.astype(jnp.float32).reshape(POPULATION_SIZE, RANK, FFN_HIDDEN)
    hidden_sum = jnp.zeros((TOKEN_TOTAL, FFN_HIDDEN), jnp.float32)
    for tensor_block in range(N_TENSOR):
        lower = tensor_block * block_span_width
        token_columns = tokens[:, lower:lower + block_span_width]
        left_cols = left_factors[:, lower:lower + block_span_width]
        base_term = jnp.dot(token_columns, up_weight[lower:lower + block_span_width, :], preferred_element_type=jnp.float32)
        up_projection = jnp.einsum("uzg,uig->uzi", token_columns.astype(jnp.float32).reshape(POPULATION_SIZE, MEMBER_TOKENS, block_span_width),
                                left_cols.astype(jnp.float32).reshape(POPULATION_SIZE, RANK, block_span_width)).astype(jnp.bfloat16)
        lowrank_correction = jnp.einsum("djt,dty->djy", up_projection.astype(jnp.float32), right_factor_wide).reshape(TOKEN_TOTAL, FFN_HIDDEN)
        partial_value = (base_term + mixing * lowrank_correction).astype(jnp.bfloat16)
        hidden_sum = hidden_sum + partial_value.astype(jnp.float32)
    hidden = hidden_sum.astype(jnp.bfloat16)
    fit_rows = jnp.repeat(fitness, RANK)
    weighted = (fit_rows[:, None] * left_factors.astype(jnp.float32)).astype(jnp.bfloat16)
    gradient = jnp.dot(weighted.T, right_factors, preferred_element_type=jnp.float32)
    gradient = gradient * (1.0 / (POPULATION_SIZE * noise_scale * RANK ** 0.5))
    return hidden, gradient.astype(jnp.bfloat16)
```

```python
import functools

import jax
import jax.numpy as jnp
from jax import lax
from jax.experimental import pallas as pl
from jax.experimental.pallas import tpu as pltpu
from jax.sharding import PartitionSpec as P

D = 5120
RANK = 4
MEMBER_TOKENS = 16
MESH = pl.DeviceIdType.MESH
NT = (((1,), (1,)), ((), ()))
TN = (((0,), (0,)), ((), ()))


def plain_body(tokens, up_weight, left_factors, right_factors, fitness):
    noise_scale = 0.25 * D ** (-0.5)
    mixing = noise_scale * RANK ** (-0.5)
    width = tokens.shape[1]
    columns = up_weight.shape[1]
    right_all = lax.all_gather(right_factors, "tensor", axis=0, tiled=True)
    members = right_all.shape[0] // RANK
    left_all = lax.all_gather(left_factors, "member", axis=0, tiled=True)
    all_tokens = lax.all_gather(tokens, "member", axis=0, tiled=True)
    projection = jnp.einsum(
        "uzg,uig->uzi",
        all_tokens.reshape(members, MEMBER_TOKENS, width),
        left_all.reshape(members, RANK, width),
        preferred_element_type=jnp.float32,
    ).astype(jnp.bfloat16)
    base = jnp.dot(all_tokens, up_weight, preferred_element_type=jnp.float32)
    correction = jnp.einsum(
        "djt,dty->djy",
        projection,
        right_all.reshape(members, RANK, columns),
        preferred_element_type=jnp.float32,
    ).reshape(base.shape)
    summed = lax.psum_scatter(
        (base + mixing * correction).astype(jnp.bfloat16), "tensor", scatter_dimension=0, tiled=True
    )
    fit_rows = jnp.repeat(fitness, RANK)
    weighted = (fit_rows[:, None] * left_all.astype(jnp.float32)).astype(jnp.bfloat16)
    gradient = jnp.einsum("kd,kf->df", weighted, right_all, preferred_element_type=jnp.float32)
    gradient = gradient * (1.0 / (members * noise_scale * RANK**0.5))
    return (summed, gradient.astype(jnp.bfloat16))


ACROSS_X = {"c": "x", "x": "c", "y": "d", "d": "y"}
ACROSS_Y = {"c": "y", "y": "c", "x": "d", "d": "x"}
LINKS = {
    "Ex": ("E", "E", "x"), "Ey": ("E", "E", "y"), "Eu": ("E", "M", "u"), "Mv": ("M", "E", "v"),
    "Mu": ("M", "M", "u"), "Mx": ("M", "M", "x"), "My": ("M", "M", "y"),
}
OWN = {"E": 0, "M": 1}
BASE = {
    "Ex": {"x": 1.4, "d": 3.8},
    "Ey": {"y": -0.5, "d": 1.5},
    "Eu": {"c": 2.7, "x": 6.3, "y": 7.2, "d": 2.4},
    "Mv": {"c": 0.4, "d": 1.7},
    "Mu": {"c": 1.2, "x": 4.0, "y": 13.7, "d": 1.4},
    "Mx": {"x": -4.0, "d": -0.1},
    "My": {"y": -5.1, "d": -3.1},
}
RANKS = {"E": (-3.6, 1.3, 2.8, 3.7), "M": (2.5, -5.9, 0.2, 2.7)}
LAYER_WEIGHT, PART_WEIGHT, LEFT_FIRST = 0.8, -0.08, 6.0
CUTS = (0, 4, 8, 10)
ORDER_E, ORDER_M = (0, 1, 2, 3), (1, 2, 0, 3)
LEAD = 2.0
COMPUTE = True


def JOBS(parts):
    every = tuple(range(1, parts + 1))
    early = [[("main", g, every)] for g in range(3)]
    late = [("main", 3, every[:-1]), ("main", 3, every[-1:])]
    return early[0] + [("weigh",)] + [("grad", j) for j in range(5)] + early[1] + early[2] + late


BYTES_PER_US = 98.5e3 / 2
HOP_US = 1.6


def landed_as(link, layer, kind):
    if link[1] == "x":
        return layer, ACROSS_X[kind]
    if link[1] == "y":
        return layer, ACROSS_Y[kind]
    return (3 - layer if link == "Mu" else layer), kind


def plan_links(sizes):
    parts = range(len(sizes))
    have = {c: {(OWN[c], "c", p): 0.0 for p in parts} for c in OWN}
    claimed = {c: set(have[c]) for c in OWN}
    free = {link: 0.0 for link in LINKS}
    log, times = [], {0.0}
    while any(len(claimed[c]) < 16 * len(sizes) for c in OWN):
        now = min(times)
        times = {t for t in times if t > now + 1e-6}
        for link, (src, dst, _) in LINKS.items():
            if free[link] > now + 1e-6:
                continue
            choices = []
            for (layer, kind, p), at in have[src].items():
                there = landed_as(link, layer, kind) + (p,)
                base = BASE[link].get(there[1])
                if at > now + 1e-6 or there in claimed[dst] or base is None:
                    continue
                score = base + LAYER_WEIGHT * RANKS[dst][there[0]] + PART_WEIGHT * p - (LEFT_FIRST if p == 0 else 0)
                choices.append((round(score, 6), len(choices), (layer, kind, p), there))
            if choices:
                _, _, here, there = min(choices)
                free[link] = now + sizes[here[2]] / BYTES_PER_US
                lands = free[link] + HOP_US
                claimed[dst].add(there)
                have[dst][there] = lands
                log.append((now, link, here, there, lands))
                times |= {free[link], lands}
    return log


def plan_core(cls, log, slots, lead=LEAD):
    lands = {there: at for _, link, _, there, at in log if LINKS[link][1] == cls}
    lands.update({(OWN[cls], "c", p): 0.0 for p in range(16)})
    sends = sorted(
        (max(lands[here], start - lead), n, link, here)
        for n, (start, link, here, _, _) in enumerate(log) if LINKS[link][0] == cls
    )
    now, before, todo = 0.0, [], []
    for needs, took in slots[cls]:
        ready = max([lands[need] for need in needs], default=0.0)
        while sends and sends[0][0] <= max(now, ready):
            at, _, link, here = sends.pop(0)
            now = max(now, at) + 0.05
            todo.append((LINKS[link][2], here))
        now = max(now, ready) + took
        before.append((todo, needs))
        todo = []
    before.append((todo + [(LINKS[s[2]][2], s[3]) for s in sends], []))
    return before


def tile_of(n, step, most):
    best = step
    for size in range(step, most + 1, step):
        if n % size == 0:
            best = size
    return best


def gather_kernel(
    mixing, scale, spans,
    tok_in, w_in, left_in, right_in, fit_in,
    grad_ref, own_ref, got_ref,
    tok, left, w, rall, acc, pacc, rt, rt_layer, lpad, wl, fit,
    send_sem, recv_sem, local_sem, r_send, r_recv, p_send, p_recv,
):
    m = lax.axis_index("member")
    t = lax.axis_index("tensor")
    z, y, x = m // 4, (m // 2) % 2, m % 2
    rows, width = tok_in.shape
    facts = left_in.shape[0]
    pad = wl.shape[0] // 16
    low = lpad.shape[0]
    ftotal = w.shape[0]
    far = z >= 2
    toward = jnp.where(far, -1, 1)
    where_am_i = {"E": (z == 0) | (z == 3), "M": (z == 1) | (z == 2)}

    def at(l, yy, xx):
        return 4 * l + 2 * yy + xx

    def real(layer):
        return jnp.where(far, 3 - layer, layer)

    def member_of(kind, layer):
        return at(real(layer), 1 - y if kind in "yd" else y, 1 - x if kind in "xd" else x)

    peers = {"x": at(z, y, 1 - x), "y": at(z, 1 - y, x), "u": m + 4 * toward, "v": m - 4 * toward}
    hops = {"E": "xyu", "M": "xyuv"}

    barrier = pltpu.get_barrier_semaphore()
    pl.semaphore_signal(barrier, inc=1, device_id=(m, 1 - t), device_id_type=MESH)
    for cls in "EM":
        @pl.when(where_am_i[cls])
        def _(cls=cls):
            for d in hops[cls]:
                pl.semaphore_signal(barrier, inc=1, device_id=(peers[d], t), device_id_type=MESH)
            pl.semaphore_wait(barrier, 1 + len(hops[cls]))

    def piece_ref(who, part, own=False):
        if part == 0:
            return left_in if own else left.at[who]
        start, size = spans[part - 1]
        return (tok_in if own else tok.at[who]).at[:, pl.ds(start, size)]

    counts = {"E": [], "M": []}
    seen = {"E": set(), "M": set()}

    def copy_of(cls, slot, direction, piece):
        layer, kind, part = piece
        who = member_of(kind, layer)
        return pltpu.make_async_remote_copy(
            src_ref=piece_ref(who, part, own=(layer, kind) == (OWN[cls], "c")),
            dst_ref=piece_ref(who, part),
            send_sem=send_sem.at[slot],
            recv_sem=recv_sem.at[who, part],
            device_id=(peers[direction], t),
            device_id_type=MESH,
        )

    def arrive(cls, piece):
        layer, kind, part = piece
        if (layer, kind) == (OWN[cls], "c") or piece in seen[cls]:
            return
        seen[cls].add(piece)
        who = member_of(kind, layer)
        ref = piece_ref(who, part)
        pltpu.make_async_copy(ref, ref, recv_sem.at[who, part]).wait()

    def send(cls, direction, piece):
        arrive(cls, piece)
        copy_of(cls, len(counts[cls]), direction, piece).start()
        counts[cls].append((direction, piece))

    ft = tile_of(ftotal, 16, 448)
    tiles = ftotal // ft
    halves = p_send.shape[1] if tiles % p_send.shape[1] == 0 else 1
    order = {"E": ORDER_E, "M": ORDER_M}
    jobs = [("right",)]
    for name in JOBS(len(spans)):
        if name[0] == "main":
            jobs += [name + (h,) for h in range(halves)]
        else:
            jobs.append(name)
    gtile = tile_of(width, 128, 512)

    def needs_of(cls, job):
        if job[0] == "main":
            layer = order[cls][job[1]]
            return [(layer, kind, p) for kind in "cxyd" for p in (0, *job[2])]
        if job[0] == "weigh":
            return [(layer, kind, 0) for layer in range(4) for kind in "cxyd"]
        return []

    def took(job):
        if job[0] == "main":
            return 0.2 + 3.1 / halves * sum(spans[p - 1][1] for p in job[2]) / width
        return {"right": 3.0, "weigh": 0.6, "grad": 1.3}[job[0]]

    slots = {cls: [(needs_of(cls, job), took(job)) for job in jobs] for cls in "EM"}
    sizes = [facts * width * 2] + [rows * size * 2 for _, size in spans]
    log = plan_links(sizes)
    todo = {cls: plan_core(cls, log, slots) for cls in "EM"}

    local = [
        pltpu.make_async_copy(right_in, rall.at[t], local_sem.at[0]),
        pltpu.make_async_copy(tok_in, tok.at[m].at[:, pl.ds(0, width)], local_sem.at[1]),
        pltpu.make_async_copy(left_in, left.at[m], local_sem.at[2]),
        pltpu.make_async_copy(fit_in, fit, local_sem.at[3]),
        pltpu.make_async_copy(w_in, w.at[:, pl.ds(0, width)], local_sem.at[4]),
    ]
    r_copy = pltpu.make_async_remote_copy(
        src_ref=right_in, dst_ref=rall.at[t], send_sem=r_send, recv_sem=r_recv,
        device_id=(m, 1 - t), device_id_type=MESH,
    )

    def do_right():
        kk = lax.broadcasted_iota(jnp.int32, (2 * rall.shape[1], 16 * pad), 0)
        qq = lax.broadcasted_iota(jnp.int32, (2 * rall.shape[1], 16 * pad), 1)
        slot_q = qq % pad
        spread = jnp.where((slot_q < facts) & (kk == facts * (qq // pad) + slot_q), 1.0, 0.0)
        spread = spread.astype(jnp.bfloat16)
        local[0].wait()
        r_copy.wait()
        r_val = jnp.concatenate([rall[0], rall[1]], axis=0)
        rt[...] = lax.dot_general(
            r_val, spread, TN, preferred_element_type=jnp.float32
        ).astype(jnp.bfloat16)
        kk = lax.broadcasted_iota(jnp.int32, (2 * rall.shape[1], 4 * low), 0)
        qq = lax.broadcasted_iota(jnp.int32, (2 * rall.shape[1], 4 * low), 1)
        slot_q = qq % pad
        chip = 4 * (qq // low) + (qq % (4 * pad)) // pad
        spread = jnp.where((slot_q < facts) & (kk == facts * chip + slot_q), 1.0, 0.0).astype(jnp.bfloat16)
        by_layer = lax.dot_general(r_val, spread, TN, preferred_element_type=jnp.float32).astype(jnp.bfloat16)
        for l in range(4):
            rt_layer[l] = by_layer[:, l * low:(l + 1) * low]

    def padded(value):
        if facts < pad:
            value = jnp.concatenate([value, jnp.zeros((pad - facts, width), value.dtype)], axis=0)
        return value

    def do_weigh():
        slot_row = lax.broadcasted_iota(jnp.int32, (pad, 1), 0) // RANK
        for b in range(16):
            col = jnp.zeros((pad, 1), jnp.float32)
            for r in range(facts // RANK):
                col = jnp.where(slot_row == r, fit[b * (facts // RANK) + r], col)
            wl[pl.ds(b * pad, pad), :] = (padded(left[b]).astype(jnp.float32) * col).astype(jnp.bfloat16)

    def do_grad(j):
        @pl.loop(0, tiles)
        def _(i):
            fspan = pl.ds(pl.multiple_of(i * ft, 16), ft)
            g = jnp.dot(rt[fspan, :], wl[:, j * gtile:(j + 1) * gtile], preferred_element_type=jnp.float32)
            grad_ref[fspan, j * gtile:(j + 1) * gtile] = (g * scale).astype(jnp.bfloat16)

    def exchange(side, piece):
        span = pl.ds(piece * (ftotal // halves), ftotal // halves)
        return pltpu.make_async_remote_copy(
            src_ref=own_ref.at[2 + side].at[span], dst_ref=got_ref.at[side].at[span],
            send_sem=p_send.at[side, piece], recv_sem=p_recv.at[side, piece],
            device_id=(m, 1 - t), device_id_type=MESH,
        )

    group = 4 * rows

    def do_main(step, parts, half):
        l = real(jnp.where(where_am_i["E"], order["E"][step], order["M"][step]))
        side = l % 2
        mine_here = l // 2 == t
        first, last = parts[0] == 1, parts[-1] == len(spans)
        begin, end = spans[parts[0] - 1][0], sum(spans[parts[-1] - 1])
        layer = pl.ds(4 * l, 4)
        if half == 0:
            if first:
                for i in range(4):
                    value = padded(left[4 * l + i])
                    for copy in range(low // (4 * pad)):
                        lpad[pl.ds((4 * copy + i) * pad, pad), :] = value
            toks = tok[layer, :, begin:end].reshape(group, end - begin)
            proj = lax.dot_general(toks, lpad[:, begin:end], NT, preferred_element_type=jnp.float32)
            if not first:
                proj = pacc[...] + proj
            if not last:
                pacc[...] = proj
            else:
                rr = lax.broadcasted_iota(jnp.int32, (group, low), 0)
                qc = lax.broadcasted_iota(jnp.int32, (group, low), 1)
                sq = qc % pad
                mine = (sq < facts) & (
                    (facts // RANK) * ((qc % (4 * pad)) // pad) + sq // RANK == rr // MEMBER_TOKENS
                )
                proj = mixing * jnp.where(mine, proj, 0.0).astype(jnp.bfloat16).astype(jnp.float32)
                high = proj.astype(jnp.bfloat16)
                rest = (proj - high.astype(jnp.float32)).astype(jnp.bfloat16)
                tok[layer, :, width:] = jnp.where(qc < 4 * pad, high, rest).reshape(4, rows, low)
                w[:, width:] = rt_layer[l]
        if last:
            end = width + low
        slot = jnp.where(mine_here, side, 2 + side)

        @pl.loop(half * (tiles // halves), (half + 1) * (tiles // halves))
        def _(i):
            span = pl.ds(pl.multiple_of(i * ft, 16), ft)
            value = lax.dot_general(
                w[span, begin:end], tok[layer, :, begin:end].reshape(group, end - begin), NT,
                preferred_element_type=jnp.float32,
            )
            if not first:
                value = acc[span, :] + value
            if last:
                own_ref[slot, span, :] = value.astype(jnp.bfloat16)
            else:
                acc[span, :] = value

        if last:
            @pl.when(jnp.logical_not(mine_here))
            def _():
                exchange(side, half).start()

    def comm(n):
        for cls in "EM":
            sends, needs = todo[cls][n]
            if n > 0 and not sends and all(need in seen[cls] for need in needs):
                continue

            @pl.when(where_am_i[cls])
            def _(cls=cls, sends=sends, needs=needs):
                for direction, piece in sends:
                    send(cls, direction, piece)
                for need in needs:
                    arrive(cls, need)

    for n, job in enumerate(jobs):
        comm(n)
        if n == 1:
            for copy in local[1:]:
                copy.wait()
        if n == 0:
            r_copy.start()
            for copy in local:
                copy.start()
            do_right()
        elif not COMPUTE:
            pass
        elif job[0] == "weigh":
            do_weigh()
        elif job[0] == "grad":
            do_grad(job[1])
        else:
            do_main(*job[1:])
    comm(len(jobs))

    for cls in "EM":
        @pl.when(where_am_i[cls])
        def _(cls=cls):
            for layer in range(4):
                for kind in "cxyd":
                    for part in range(len(spans) + 1):
                        arrive(cls, (layer, kind, part))
            for slot, (direction, piece) in enumerate(counts[cls]):
                copy_of(cls, slot, direction, piece).wait_send()
    if COMPUTE:
        for side in range(2):
            for piece in range(halves):
                exchange(side, piece).wait()


def finish_kernel(grad, own, got, h_ref, g_ref, hv, g_sem, h_sem):
    columns = own.shape[1]
    n = own.shape[2]
    gp, hp = g_sem.shape[0], h_sem.shape[0]

    def copy(src, dst, sem, pieces, i):
        span = pl.ds(i * (columns // pieces), columns // pieces)
        return pltpu.make_async_copy(src.at[span], dst.at[span], sem.at[i])

    for i in range(gp):
        copy(grad, g_ref, g_sem, gp, i).start()
    for i in range(hp):
        span = pl.ds(i * (columns // hp), columns // hp)
        for side in range(2):
            total = own[side, span, :].astype(jnp.float32) + got[side, span, :].astype(jnp.float32)
            hv[span, side * n:(side + 1) * n] = total.astype(jnp.bfloat16)
        copy(hv, h_ref, h_sem, hp, i).start()
    for i in range(gp):
        copy(grad, g_ref, g_sem, gp, i).wait()
    for i in range(hp):
        copy(hv, h_ref, h_sem, hp, i).wait()


def body(tokens, up_weight, left_factors, right_factors, fitness):
    noise_scale = 0.25 * D ** (-0.5)
    mixing = noise_scale * RANK ** (-0.5)
    rows, width = tokens.shape
    facts = left_factors.shape[0]
    columns = up_weight.shape[1]
    rrows = right_factors.shape[0]
    pad = -(-facts // 16) * 16
    members = fitness.shape[0]
    bf, f32 = jnp.bfloat16, jnp.float32
    hbm = pl.BlockSpec(memory_space=pltpu.HBM)
    vm = pl.BlockSpec(memory_space=pltpu.VMEM)
    dma = pltpu.SemaphoreType.DMA
    edges = [width * n // 10 // 128 * 128 for n in CUTS]
    spans = [(a, b - a) for a, b in zip(edges, edges[1:])]
    scale = 1.0 / (members * noise_scale * RANK**0.5)
    grad, own, got = pl.pallas_call(
        functools.partial(gather_kernel, mixing, scale, spans),
        out_shape=(
            jax.ShapeDtypeStruct((columns, width), bf),
            jax.ShapeDtypeStruct((4, columns, 4 * rows), bf),
            jax.ShapeDtypeStruct((2, columns, 4 * rows), bf),
        ),
        in_specs=[hbm] * 5,
        out_specs=(vm, vm, vm),
        scratch_shapes=[
            pltpu.VMEM((16, rows, width + 8 * pad), bf),
            pltpu.VMEM((16, facts, width), bf),
            pltpu.VMEM((columns, width + 8 * pad), bf),
            pltpu.VMEM((2, rrows, columns), bf),
            pltpu.VMEM((columns, 4 * rows), f32),
            pltpu.VMEM((4 * rows, 8 * pad), f32),
            pltpu.VMEM((columns, 16 * pad), bf),
            pltpu.VMEM((4, columns, 8 * pad), bf),
            pltpu.VMEM((8 * pad, width), bf),
            pltpu.VMEM((16 * pad, width), bf),
            pltpu.SMEM((members,), f32),
            dma((40 * (1 + len(spans)),)), dma((16, 1 + len(spans))), dma((5,)), dma, dma, dma((2, 2)), dma((2, 2)),
        ],
        compiler_params=pltpu.CompilerParams(
            collective_id=0, has_side_effects=True, vmem_limit_bytes=28 * 1024 * 1024
        ),
        name="gather_project",
    )(
        pltpu.with_memory_space_constraint(tokens, pltpu.HBM),
        pltpu.with_memory_space_constraint(up_weight.T, pltpu.HBM),
        pltpu.with_memory_space_constraint(left_factors, pltpu.HBM),
        pltpu.with_memory_space_constraint(right_factors, pltpu.HBM),
        pltpu.with_memory_space_constraint(fitness, pltpu.HBM),
    )
    pieces = 4 if columns % 64 == 0 else 1
    hidden, gradient = pl.pallas_call(
        finish_kernel,
        out_shape=(
            jax.ShapeDtypeStruct((columns, 8 * rows), bf),
            jax.ShapeDtypeStruct((columns, width), bf),
        ),
        in_specs=[vm, vm, vm],
        out_specs=(hbm, hbm),
        scratch_shapes=[pltpu.VMEM((columns, 8 * rows), bf), dma((pieces,)), dma((pieces,))],
        compiler_params=pltpu.CompilerParams(vmem_limit_bytes=8 * 1024 * 1024),
        name="finish",
    )(grad, own, got)
    return hidden.T, gradient.T


def solution(mesh):
    fits = mesh.shape["member"] == 16 and mesh.shape["tensor"] == 2
    return jax.shard_map(
        body if fits else plain_body,
        mesh=mesh,
        in_specs=(
            P("member", "tensor"),
            P("tensor", "member"),
            P("member", "tensor"),
            P("tensor", "member"),
            P(),
        ),
        out_specs=(P("tensor", "member"), P("tensor", "member")),
        check_vma=False,
    )
```

```python
import functools

import jax
import jax.numpy as jnp
from jax import lax
from jax.experimental import pallas as pl
from jax.experimental.pallas import tpu as pltpu
from jax.sharding import PartitionSpec as P

D = 5120
RANK = 4
MEMBER_TOKENS = 16
MESH = pl.DeviceIdType.MESH
NT = (((1,), (1,)), ((), ()))
TN = (((0,), (0,)), ((), ()))


def plain_body(tokens, up_weight, left_factors, right_factors, fitness):
    noise_scale = 0.25 * D ** (-0.5)
    mixing = noise_scale * RANK ** (-0.5)
    width = tokens.shape[1]
    columns = up_weight.shape[1]
    right_all = lax.all_gather(right_factors, "tensor", axis=0, tiled=True)
    members = right_all.shape[0] // RANK
    left_all = lax.all_gather(left_factors, "member", axis=0, tiled=True)
    all_tokens = lax.all_gather(tokens, "member", axis=0, tiled=True)
    projection = jnp.einsum(
        "uzg,uig->uzi",
        all_tokens.reshape(members, MEMBER_TOKENS, width),
        left_all.reshape(members, RANK, width),
        preferred_element_type=jnp.float32,
    ).astype(jnp.bfloat16)
    base = jnp.dot(all_tokens, up_weight, preferred_element_type=jnp.float32)
    correction = jnp.einsum(
        "djt,dty->djy",
        projection,
        right_all.reshape(members, RANK, columns),
        preferred_element_type=jnp.float32,
    ).reshape(base.shape)
    summed = lax.psum_scatter(
        (base + mixing * correction).astype(jnp.bfloat16), "tensor", scatter_dimension=0, tiled=True
    )
    fit_rows = jnp.repeat(fitness, RANK)
    weighted = (fit_rows[:, None] * left_all.astype(jnp.float32)).astype(jnp.bfloat16)
    gradient = jnp.einsum("kd,kf->df", weighted, right_all, preferred_element_type=jnp.float32)
    gradient = gradient * (1.0 / (members * noise_scale * RANK**0.5))
    return (summed, gradient.astype(jnp.bfloat16))


ACROSS_X = {"c": "x", "x": "c", "y": "d", "d": "y"}
ACROSS_Y = {"c": "y", "y": "c", "x": "d", "d": "x"}
LINKS = {
    "Ex": ("E", "E", "x"), "Ey": ("E", "E", "y"), "Eu": ("E", "M", "u"), "Mv": ("M", "E", "v"),
    "Mu": ("M", "M", "u"), "Mx": ("M", "M", "x"), "My": ("M", "M", "y"),
}
OWN = {"E": 0, "M": 1}
BASE = {
    "Ex": {"x": -0.4, "d": 2.7},
    "Ey": {"y": 4.4, "d": 0.4},
    "Eu": {"c": 1.1, "x": 5.0, "y": 2.5, "d": 3.0},
    "Mv": {"c": 2.4, "d": 5.1},
    "Mu": {"c": -1.3, "x": 5.3, "y": 13.1, "d": -0.8},
    "Mx": {"x": 0.0, "d": 3.8},
    "My": {"y": -1.4, "d": -0.5},
}
RANKS = {"E": (-6.9, 0.7, 2.6, 3.9), "M": (1.8, -6.3, 5.0, 6.2)}
LAYER_WEIGHT, PART_WEIGHT, LEFT_FIRST = 1.0, 0.12, 7.7
CUTS = (0, 5, 10)
ORDER_E, ORDER_M = (0, 1, 2, 3), (1, 0, 2, 3)
LEAD = 2.0
COMPUTE = True


def JOBS(parts):
    every = tuple(range(1, parts + 1))
    early = [[("main", g, every)] for g in range(3)]
    late = [("main", 3, every[:-1]), ("main", 3, every[-1:])]
    return early[0] + [("weigh",)] + [("grad", j) for j in range(4)] + early[1] + early[2] + late


RIGHT_AT = 2.5
GRAD_ROWS, GRAD_COLS = 432, 1280
BYTES_PER_US = 85e3 / 2
HOP_US = 2.0


def landed_as(link, layer, kind):
    if link[1] == "x":
        return layer, ACROSS_X[kind]
    if link[1] == "y":
        return layer, ACROSS_Y[kind]
    return (3 - layer if link == "Mu" else layer), kind


def plan_links(sizes):
    parts = range(len(sizes))
    have = {c: {(OWN[c], "c", p): 0.0 for p in parts} for c in OWN}
    claimed = {c: set(have[c]) for c in OWN}
    free = {link: 0.0 for link in LINKS}
    log, times = [], {0.0}
    while any(len(claimed[c]) < 16 * len(sizes) for c in OWN):
        now = min(times)
        times = {t for t in times if t > now + 1e-6}
        for link, (src, dst, _) in LINKS.items():
            if free[link] > now + 1e-6:
                continue
            choices = []
            for (layer, kind, p), at in have[src].items():
                there = landed_as(link, layer, kind) + (p,)
                base = BASE[link].get(there[1])
                if at > now + 1e-6 or there in claimed[dst] or base is None:
                    continue
                score = base + LAYER_WEIGHT * RANKS[dst][there[0]] + PART_WEIGHT * p - (LEFT_FIRST if p == 0 else 0)
                choices.append((round(score, 6), len(choices), (layer, kind, p), there))
            if choices:
                _, _, here, there = min(choices)
                free[link] = now + sizes[here[2]] / BYTES_PER_US
                lands = free[link] + HOP_US
                claimed[dst].add(there)
                have[dst][there] = lands
                log.append((now, link, here, there, lands))
                times |= {free[link], lands}
    return log


def plan_core(cls, log, slots, lead=LEAD):
    lands = {there: at for _, link, _, there, at in log if LINKS[link][1] == cls}
    lands.update({(OWN[cls], "c", p): 0.0 for p in range(16)})
    sends = sorted(
        (max(lands[here], start - lead), n, link, here)
        for n, (start, link, here, _, _) in enumerate(log) if LINKS[link][0] == cls
    )
    now, before, todo = 0.0, [], []
    for needs, took, _ in slots[cls]:
        ready = max([lands[need] for need in needs], default=0.0)
        while sends and sends[0][0] <= max(now, ready):
            at, _, link, here = sends.pop(0)
            now = max(now, at) + 0.05
            todo.append((LINKS[link][2], here))
        now = max(now, ready) + took
        before.append((todo, needs))
        todo = []
    before.append((todo + [(LINKS[s[2]][2], s[3]) for s in sends], []))
    return before


def tile_of(n, step, most):
    best = step
    for size in range(step, most + 1, step):
        if n % size == 0:
            best = size
    return best


def gather_kernel(
    mixing, scale, spans,
    tok_in, w_in, left_in, right_in, fit_in,
    grad_ref, own_ref, got_ref,
    tok, left, w, rall, acc, rt, wl, fit,
    send_sem, recv_sem, local_sem, r_send, r_recv, p_send, p_recv, step_sem,
):
    m = lax.axis_index("member")
    t = lax.axis_index("tensor")
    z, y, x = m // 4, (m // 2) % 2, m % 2
    rows, width = tok_in.shape
    facts = left_in.shape[0]
    pad = wl.shape[0] // 16
    ftotal = w_in.shape[0]
    low = w.shape[0] - ftotal
    far = z >= 2
    toward = jnp.where(far, -1, 1)
    where_am_i = {"E": (z == 0) | (z == 3), "M": (z == 1) | (z == 2)}

    def at(l, yy, xx):
        return 4 * l + 2 * yy + xx

    def real(layer):
        return jnp.where(far, 3 - layer, layer)

    def member_of(kind, layer):
        return at(real(layer), 1 - y if kind in "yd" else y, 1 - x if kind in "xd" else x)

    peers = {"x": at(z, y, 1 - x), "y": at(z, 1 - y, x), "u": m + 4 * toward, "v": m - 4 * toward}
    hops = {"E": "xyu", "M": "xyuv"}

    barrier = pltpu.get_barrier_semaphore()
    pl.semaphore_signal(barrier, inc=1, device_id=(m, 1 - t), device_id_type=MESH)
    for cls in "EM":
        @pl.when(where_am_i[cls])
        def _(cls=cls):
            for d in hops[cls]:
                pl.semaphore_signal(barrier, inc=1, device_id=(peers[d], t), device_id_type=MESH)
            pl.semaphore_wait(barrier, 1 + len(hops[cls]))

    def piece_ref(who, part, own=False):
        if part == 0:
            return left_in if own else left.at[who]
        start, size = spans[part - 1]
        return (tok_in if own else tok.at[who]).at[:, pl.ds(start, size)]

    counts = {"E": [], "M": []}
    seen = {"E": set(), "M": set()}

    def copy_of(cls, slot, direction, piece):
        layer, kind, part = piece
        who = member_of(kind, layer)
        return pltpu.make_async_remote_copy(
            src_ref=piece_ref(who, part, own=(layer, kind) == (OWN[cls], "c")),
            dst_ref=piece_ref(who, part),
            send_sem=send_sem.at[slot],
            recv_sem=recv_sem.at[who, part],
            device_id=(peers[direction], t),
            device_id_type=MESH,
        )

    def arrive(cls, piece):
        layer, kind, part = piece
        if (layer, kind) == (OWN[cls], "c") or piece in seen[cls]:
            return
        seen[cls].add(piece)
        who = member_of(kind, layer)
        ref = piece_ref(who, part)
        pltpu.make_async_copy(ref, ref, recv_sem.at[who, part]).wait()

    def send(cls, direction, piece):
        arrive(cls, piece)
        copy_of(cls, len(counts[cls]), direction, piece).start()
        counts[cls].append((direction, piece))

    halves = p_send.shape[1]
    ft = ftotal // halves
    rt_rows = tile_of(ft, 16, 448)
    order = {"E": ORDER_E, "M": ORDER_M}
    jobs = [("start",), ("right",)]
    for name in JOBS(len(spans)):
        if name[0] == "main":
            jobs += [name + (h,) for h in range(halves)]
        else:
            jobs.append(name)
    gft = tile_of(ftotal, 16, GRAD_ROWS)
    gtile = tile_of(width, 128, GRAD_COLS)

    def needs_of(cls, job):
        if job[0] == "main":
            layer = order[cls][job[1]]
            return [(layer, kind, p) for kind in "cxyd" for p in (0, *job[2])]
        if job[0] == "weigh":
            return [(layer, kind, 0) for layer in range(4) for kind in "cxyd"]
        return []

    def took(job):
        if job[0] == "main":
            return 0.2 + 3.1 / halves * sum(spans[p - 1][1] for p in job[2]) / width
        return {"start": 0.2, "right": 2.5, "weigh": 0.6, "grad": 1.4}[job[0]]

    slots = {cls: [(needs_of(cls, job), took(job), RIGHT_AT if job[0] == "right" else 0.0) for job in jobs] for cls in "EM"}
    sizes = [facts * width * 2] + [rows * size * 2 for _, size in spans]
    log = plan_links(sizes)
    todo = {cls: plan_core(cls, log, slots) for cls in "EM"}

    local = [
        pltpu.make_async_copy(right_in, rall.at[t], local_sem.at[0]),
        pltpu.make_async_copy(tok_in, tok.at[m].at[:, pl.ds(0, width)], local_sem.at[1]),
        pltpu.make_async_copy(left_in, left.at[m], local_sem.at[2]),
        pltpu.make_async_copy(fit_in, fit, local_sem.at[3]),
        pltpu.make_async_copy(w_in, w.at[pl.ds(low, ftotal), pl.ds(0, width)], local_sem.at[4]),
    ]
    r_copy = pltpu.make_async_remote_copy(
        src_ref=right_in, dst_ref=rall.at[t], send_sem=r_send, recv_sem=r_recv,
        device_id=(m, 1 - t), device_id_type=MESH,
    )

    def do_right():
        kk = lax.broadcasted_iota(jnp.int32, (2 * rall.shape[1], 16 * pad), 0)
        qq = lax.broadcasted_iota(jnp.int32, (2 * rall.shape[1], 16 * pad), 1)
        slot_q = qq % pad
        spread = jnp.where((slot_q < facts) & (kk == facts * (qq // pad) + slot_q), 1.0, 0.0)
        spread = spread.astype(jnp.bfloat16)
        local[0].wait()
        r_copy.wait()
        r_val = jnp.concatenate([rall[0], rall[1]], axis=0)
        rt[...] = lax.dot_general(
            r_val, spread, TN, preferred_element_type=jnp.float32
        ).astype(jnp.bfloat16)

    def padded(value):
        if facts < pad:
            value = jnp.concatenate([value, jnp.zeros((pad - facts, width), value.dtype)], axis=0)
        return value

    def do_weigh():
        slot_row = lax.broadcasted_iota(jnp.int32, (pad, 1), 0) // RANK
        for b in range(16):
            col = jnp.zeros((pad, 1), jnp.float32)
            for r in range(facts // RANK):
                col = jnp.where(slot_row == r, fit[b * (facts // RANK) + r], col)
            wl[pl.ds(b * pad, pad), :] = (padded(left[b]).astype(jnp.float32) * col).astype(jnp.bfloat16)

    def do_grad(i):
        @pl.loop(0, width // gtile)
        def _(j):
            dspan = pl.ds(pl.multiple_of(j * gtile, 128), gtile)
            g = jnp.dot(rt[i * gft:(i + 1) * gft, :], wl[:, dspan], preferred_element_type=jnp.float32)
            grad_ref[i * gft:(i + 1) * gft, dspan] = (g * scale).astype(jnp.bfloat16)

    def exchange(side, piece):
        span = pl.ds(piece * (ftotal // halves), ftotal // halves)
        return pltpu.make_async_remote_copy(
            src_ref=own_ref.at[2 + side].at[span], dst_ref=got_ref.at[side].at[span],
            send_sem=p_send.at[side, piece], recv_sem=p_recv.at[side, piece],
            device_id=(m, 1 - t), device_id_type=MESH,
        )

    group = 4 * rows

    def do_main(step, parts, half):
        l = real(jnp.where(where_am_i["E"], order["E"][step], order["M"][step]))
        side = l % 2
        mine_here = l // 2 == t
        first, last = parts[0] == 1, parts[-1] == len(spans)
        begin, end = spans[parts[0] - 1][0], sum(spans[parts[-1] - 1])
        layer = pl.ds(4 * l, 4)
        inner = low // 2
        slot = jnp.where(mine_here, side, 2 + side)
        if first and half == 0:
            here = inner * (l % 2)
            w[pl.ds(pl.multiple_of(inner - here, 16), inner), :width] = jnp.zeros((inner, width), w.dtype)
            for i in range(4):
                w[pl.ds(pl.multiple_of(here + i * pad, 16), pad), :width] = padded(left[4 * l + i])
            pair = jnp.where(l // 2 == 0, rt[:, :low], rt[:, low:])
            w[low:, width:width + low] = pair
            w[low:, width + low:] = pair

        def dot(row, count, start, stop):
            return lax.dot_general(
                w[row:row + count, start:stop], tok[layer, :, start:stop].reshape(group, stop - start), NT,
                preferred_element_type=jnp.float32,
            )

        def tile(row, count, start, stop):
            value = lax.dot_general(
                w[pl.ds(row, count), start:stop], tok[layer, :, start:stop].reshape(group, stop - start), NT,
                preferred_element_type=jnp.float32,
            )
            return value if first else acc[pl.ds(row, count), :] + value

        if half == 0:
            value = tile(0, low + rt_rows, begin, end)
            if not last:
                acc[:low + rt_rows, :] = value
            else:
                qc = lax.broadcasted_iota(jnp.int32, (low, group), 0)
                rr = lax.broadcasted_iota(jnp.int32, (low, group), 1)
                sq = qc % pad
                mine = (qc // inner == l % 2) & (sq < facts) & (
                    (facts // RANK) * ((qc % inner) // pad) + sq // RANK == rr // MEMBER_TOKENS
                )
                proj = jnp.where(mine, value[:low], 0.0).astype(jnp.bfloat16).astype(jnp.float32)
                proj = mixing * proj.T
                high = proj.astype(jnp.bfloat16)
                rest = (proj - high.astype(jnp.float32)).astype(jnp.bfloat16)
                tok[layer, :, width:width + low] = high.reshape(4, rows, low)
                tok[layer, :, width + low:] = rest.reshape(4, rows, low)
                value = value[low:] + lax.dot_general(
                    w[low:low + rt_rows, width:], tok[layer, :, width:].reshape(group, 2 * low), NT,
                    preferred_element_type=jnp.float32,
                )
                own_ref[slot, :rt_rows, :group] = value.astype(jnp.bfloat16)

        per = ft // rt_rows

        @pl.loop(half * per + (half == 0), (half + 1) * per)
        def _(i):
            row = pl.multiple_of(i * rt_rows, 16)
            value = tile(pl.multiple_of(row + low, 16), rt_rows, begin, width + 2 * low if last else end)
            if last:
                own_ref[slot, pl.ds(row, rt_rows), :group] = value.astype(jnp.bfloat16)
            else:
                acc[pl.ds(pl.multiple_of(row + low, 16), rt_rows), :] = value

        if not last:
            return

        @pl.when(jnp.logical_not(mine_here))
        def _():
            exchange(side, half).start()

    def comm(n):
        for cls in "EM":
            sends, needs = todo[cls][n]
            if n > 0 and not sends and all(need in seen[cls] for need in needs):
                continue

            @pl.when(where_am_i[cls])
            def _(cls=cls, sends=sends, needs=needs):
                for direction, piece in sends:
                    send(cls, direction, piece)
                for need in needs:
                    arrive(cls, need)

    for n, job in enumerate(jobs):
        if n > 1:
            pl.semaphore_wait(step_sem, 1)
        comm(n)
        if 0 < n:
            pl.semaphore_signal(step_sem, inc=1, device_id=(m, 1 - t), device_id_type=MESH)
        if n == 2:
            for copy in local[1:]:
                copy.wait()
        if job[0] == "start":
            r_copy.start()
            for copy in local:
                copy.start()
        elif job[0] == "right":
            do_right()
        elif not COMPUTE:
            pass
        elif job[0] == "weigh":
            do_weigh()
        elif job[0] == "grad":
            do_grad(job[1])
        else:
            do_main(*job[1:])
    pl.semaphore_wait(step_sem, 1)
    comm(len(jobs))

    for cls in "EM":
        @pl.when(where_am_i[cls])
        def _(cls=cls):
            for layer in range(4):
                for kind in "cxyd":
                    for part in range(len(spans) + 1):
                        arrive(cls, (layer, kind, part))
            for slot, (direction, piece) in enumerate(counts[cls]):
                copy_of(cls, slot, direction, piece).wait_send()
    if COMPUTE:
        for side in range(2):
            for piece in range(halves):
                exchange(side, piece).wait()


def finish_kernel(grad, own, got, h_ref, g_ref, hv, g_sem, h_sem):
    columns = own.shape[1]
    n = hv.shape[1] // 2
    gp, hp = g_sem.shape[0], h_sem.shape[0]

    def copy(src, dst, sem, pieces, i):
        span = pl.ds(i * (columns // pieces), columns // pieces)
        return pltpu.make_async_copy(src.at[span], dst.at[span], sem.at[i])

    for i in range(gp):
        copy(grad, g_ref, g_sem, gp, i).start()
    for i in range(hp):
        span = pl.ds(i * (columns // hp), columns // hp)
        for side in range(2):
            total = own[side, span, :n].astype(jnp.float32) + got[side, span, :n].astype(jnp.float32)
            hv[span, side * n:(side + 1) * n] = total.astype(jnp.bfloat16)
        copy(hv, h_ref, h_sem, hp, i).start()
    for i in range(gp):
        copy(grad, g_ref, g_sem, gp, i).wait()
    for i in range(hp):
        copy(hv, h_ref, h_sem, hp, i).wait()


def body(tokens, up_weight, left_factors, right_factors, fitness):
    noise_scale = 0.25 * D ** (-0.5)
    mixing = noise_scale * RANK ** (-0.5)
    rows, width = tokens.shape
    facts = left_factors.shape[0]
    columns = up_weight.shape[1]
    rrows = right_factors.shape[0]
    pad = -(-facts // 16) * 16
    members = fitness.shape[0]
    bf, f32 = jnp.bfloat16, jnp.float32
    hbm = pl.BlockSpec(memory_space=pltpu.HBM)
    vm = pl.BlockSpec(memory_space=pltpu.VMEM)
    dma = pltpu.SemaphoreType.DMA
    edges = [width * n // 10 // 128 * 128 for n in CUTS]
    spans = [(a, b - a) for a, b in zip(edges, edges[1:])]
    halves = 2 if columns % 32 == 0 else 1
    lanes = -(-4 * rows // 128) * 128
    scale = 1.0 / (members * noise_scale * RANK**0.5)
    grad, own, got = pl.pallas_call(
        functools.partial(gather_kernel, mixing, scale, spans),
        out_shape=(
            jax.ShapeDtypeStruct((columns, width), bf),
            jax.ShapeDtypeStruct((4, columns, lanes), bf),
            jax.ShapeDtypeStruct((2, columns, lanes), bf),
        ),
        in_specs=[hbm] * 5,
        out_specs=(vm, vm, vm),
        scratch_shapes=[
            pltpu.VMEM((16, rows, width + 16 * pad), bf),
            pltpu.VMEM((16, facts, width), bf),
            pltpu.VMEM((8 * pad + columns, width + 16 * pad), bf),
            pltpu.VMEM((2, rrows, columns), bf),
            pltpu.VMEM((8 * pad + columns, 4 * rows), f32),
            pltpu.VMEM((columns, 16 * pad), bf),
            pltpu.VMEM((16 * pad, width), bf),
            pltpu.SMEM((members,), f32),
            dma((40 * (1 + len(spans)),)), dma((16, 1 + len(spans))), dma((5,)), dma, dma, dma((2, halves)), dma((2, halves)), pltpu.SemaphoreType.REGULAR,
        ],
        compiler_params=pltpu.CompilerParams(
            collective_id=0, has_side_effects=True, vmem_limit_bytes=28 * 1024 * 1024
        ),
        name="gather_project",
    )(
        pltpu.with_memory_space_constraint(tokens, pltpu.HBM),
        pltpu.with_memory_space_constraint(up_weight.T, pltpu.HBM),
        pltpu.with_memory_space_constraint(left_factors, pltpu.HBM),
        pltpu.with_memory_space_constraint(right_factors, pltpu.HBM),
        pltpu.with_memory_space_constraint(fitness, pltpu.HBM),
    )
    pieces = 4 if columns % 64 == 0 else 1
    hidden, gradient = pl.pallas_call(
        finish_kernel,
        out_shape=(
            jax.ShapeDtypeStruct((columns, 8 * rows), bf),
            jax.ShapeDtypeStruct((columns, width), bf),
        ),
        in_specs=[vm, vm, vm],
        out_specs=(hbm, hbm),
        scratch_shapes=[pltpu.VMEM((columns, 8 * rows), bf), dma((pieces,)), dma((pieces,))],
        compiler_params=pltpu.CompilerParams(vmem_limit_bytes=8 * 1024 * 1024),
        name="finish",
    )(grad, own, got)
    return hidden.T, gradient.T


def solution(mesh):
    fits = mesh.shape["member"] == 16 and mesh.shape["tensor"] == 2
    return jax.shard_map(
        body if fits else plain_body,
        mesh=mesh,
        in_specs=(
            P("member", "tensor"),
            P("tensor", "member"),
            P("member", "tensor"),
            P("tensor", "member"),
            P(),
        ),
        out_specs=(P("tensor", "member"), P("tensor", "member")),
        check_vma=False,
    )
```

```python
import functools

import jax
import jax.numpy as jnp
from jax import lax
from jax.experimental import pallas as pl
from jax.experimental.pallas import tpu as pltpu
from jax.sharding import PartitionSpec as P

D = 5120
RANK = 4
MEMBER_TOKENS = 16
MESH = pl.DeviceIdType.MESH
NT = (((1,), (1,)), ((), ()))
TN = (((0,), (0,)), ((), ()))


def plain_body(tokens, up_weight, left_factors, right_factors, fitness):
    noise_scale = 0.25 * D ** (-0.5)
    mixing = noise_scale * RANK ** (-0.5)
    width = tokens.shape[1]
    columns = up_weight.shape[1]
    right_all = lax.all_gather(right_factors, "tensor", axis=0, tiled=True)
    members = right_all.shape[0] // RANK
    left_all = lax.all_gather(left_factors, "member", axis=0, tiled=True)
    all_tokens = lax.all_gather(tokens, "member", axis=0, tiled=True)
    projection = jnp.einsum(
        "uzg,uig->uzi",
        all_tokens.reshape(members, MEMBER_TOKENS, width),
        left_all.reshape(members, RANK, width),
        preferred_element_type=jnp.float32,
    ).astype(jnp.bfloat16)
    base = jnp.dot(all_tokens, up_weight, preferred_element_type=jnp.float32)
    correction = jnp.einsum(
        "djt,dty->djy",
        projection,
        right_all.reshape(members, RANK, columns),
        preferred_element_type=jnp.float32,
    ).reshape(base.shape)
    summed = lax.psum_scatter(
        (base + mixing * correction).astype(jnp.bfloat16), "tensor", scatter_dimension=0, tiled=True
    )
    fit_rows = jnp.repeat(fitness, RANK)
    weighted = (fit_rows[:, None] * left_all.astype(jnp.float32)).astype(jnp.bfloat16)
    gradient = jnp.einsum("kd,kf->df", weighted, right_all, preferred_element_type=jnp.float32)
    gradient = gradient * (1.0 / (members * noise_scale * RANK**0.5))
    return (summed, gradient.astype(jnp.bfloat16))


ACROSS_X = {"c": "x", "x": "c", "y": "d", "d": "y"}
ACROSS_Y = {"c": "y", "y": "c", "x": "d", "d": "x"}
LINKS = {
    "Ex": ("E", "E", "x"), "Ey": ("E", "E", "y"), "Eu": ("E", "M", "u"), "Mv": ("M", "E", "v"),
    "Mu": ("M", "M", "u"), "Mx": ("M", "M", "x"), "My": ("M", "M", "y"),
}
OWN = {"E": 0, "M": 1}
BASE = {
    "Ex": {"x": -0.4, "d": 2.7},
    "Ey": {"y": 4.4, "d": 0.4},
    "Eu": {"c": 1.1, "x": 5.0, "y": 2.5, "d": 3.0},
    "Mv": {"c": 2.4, "d": 5.1},
    "Mu": {"c": -1.3, "x": 5.3, "y": 13.1, "d": -0.8},
    "Mx": {"x": 0.0, "d": 3.8},
    "My": {"y": -1.4, "d": -0.5},
}
RANKS = {"E": (-6.9, 0.7, 2.6, 3.9), "M": (1.8, -6.3, 5.0, 6.2)}
LAYER_WEIGHT, PART_WEIGHT, LEFT_FIRST = 1.0, 0.12, 7.7
CUTS = (0, 5, 10)
ORDER_E, ORDER_M = (0, 1, 2, 3), (1, 0, 2, 3)
LEAD = 2.0
COMPUTE = True


def JOBS(parts):
    every = tuple(range(1, parts + 1))
    early = [[("main", g, every)] for g in range(3)]
    late = [("main", 3, every[:-1]), ("main", 3, every[-1:])]
    return early[0] + [("weigh",)] + [("grad", j) for j in range(4)] + early[1] + [("main", 2, every[:-1]), ("main", 2, every[-1:])] + late


RIGHT_AT = 2.5
GRAD_ROWS, GRAD_COLS = 432, 1280
BYTES_PER_US = 85e3 / 2
HOP_US = 2.0


def landed_as(link, layer, kind):
    if link[1] == "x":
        return layer, ACROSS_X[kind]
    if link[1] == "y":
        return layer, ACROSS_Y[kind]
    return (3 - layer if link == "Mu" else layer), kind


def plan_links(sizes):
    parts = range(len(sizes))
    have = {c: {(OWN[c], "c", p): 0.0 for p in parts} for c in OWN}
    claimed = {c: set(have[c]) for c in OWN}
    free = {link: 0.0 for link in LINKS}
    log, times = [], {0.0}
    while any(len(claimed[c]) < 16 * len(sizes) for c in OWN):
        now = min(times)
        times = {t for t in times if t > now + 1e-6}
        for link, (src, dst, _) in LINKS.items():
            if free[link] > now + 1e-6:
                continue
            choices = []
            for (layer, kind, p), at in have[src].items():
                there = landed_as(link, layer, kind) + (p,)
                base = BASE[link].get(there[1])
                if at > now + 1e-6 or there in claimed[dst] or base is None:
                    continue
                score = base + LAYER_WEIGHT * RANKS[dst][there[0]] + PART_WEIGHT * p - (LEFT_FIRST if p == 0 else 0)
                choices.append((round(score, 6), len(choices), (layer, kind, p), there))
            if choices:
                _, _, here, there = min(choices)
                free[link] = now + sizes[here[2]] / BYTES_PER_US
                lands = free[link] + HOP_US
                claimed[dst].add(there)
                have[dst][there] = lands
                log.append((now, link, here, there, lands))
                times |= {free[link], lands}
    return log


def plan_core(cls, log, slots, lead=LEAD):
    lands = {there: at for _, link, _, there, at in log if LINKS[link][1] == cls}
    lands.update({(OWN[cls], "c", p): 0.0 for p in range(16)})
    sends = sorted(
        (max(lands[here], start - lead), n, link, here)
        for n, (start, link, here, _, _) in enumerate(log) if LINKS[link][0] == cls
    )
    now, before, todo = 0.0, [], []
    for needs, took, _ in slots[cls]:
        ready = max([lands[need] for need in needs], default=0.0)
        while sends and sends[0][0] <= max(now, ready):
            at, _, link, here = sends.pop(0)
            now = max(now, at) + 0.05
            todo.append((LINKS[link][2], here))
        now = max(now, ready) + took
        before.append((todo, needs))
        todo = []
    before.append((todo + [(LINKS[s[2]][2], s[3]) for s in sends], []))
    return before


def tile_of(n, step, most):
    best = step
    for size in range(step, most + 1, step):
        if n % size == 0:
            best = size
    return best


def gather_kernel(
    mixing, scale, spans,
    tok_in, w_in, left_in, right_in, fit_in,
    grad_ref, own_ref, got_ref,
    tok, left, w, rall, acc, rt, wl, fit,
    send_sem, recv_sem, local_sem, r_send, r_recv, p_send, p_recv, step_sem,
):
    m = lax.axis_index("member")
    t = lax.axis_index("tensor")
    z, y, x = m // 4, (m // 2) % 2, m % 2
    rows, width = tok_in.shape
    facts = left_in.shape[0]
    pad = wl.shape[0] // 16
    ftotal = w_in.shape[0]
    low = w.shape[0] - ftotal
    far = z >= 2
    toward = jnp.where(far, -1, 1)
    where_am_i = {"E": (z == 0) | (z == 3), "M": (z == 1) | (z == 2)}

    def at(l, yy, xx):
        return 4 * l + 2 * yy + xx

    def real(layer):
        return jnp.where(far, 3 - layer, layer)

    def member_of(kind, layer):
        return at(real(layer), 1 - y if kind in "yd" else y, 1 - x if kind in "xd" else x)

    peers = {"x": at(z, y, 1 - x), "y": at(z, 1 - y, x), "u": m + 4 * toward, "v": m - 4 * toward}
    hops = {"E": "xyu", "M": "xyuv"}

    barrier = pltpu.get_barrier_semaphore()
    pl.semaphore_signal(barrier, inc=1, device_id=(m, 1 - t), device_id_type=MESH)
    for cls in "EM":
        @pl.when(where_am_i[cls])
        def _(cls=cls):
            for d in hops[cls]:
                pl.semaphore_signal(barrier, inc=1, device_id=(peers[d], t), device_id_type=MESH)
            pl.semaphore_wait(barrier, 1 + len(hops[cls]))

    def piece_ref(who, part, own=False):
        if part == 0:
            return left_in if own else left.at[who]
        start, size = spans[part - 1]
        return (tok_in if own else tok.at[who]).at[:, pl.ds(start, size)]

    counts = {"E": [], "M": []}
    seen = {"E": set(), "M": set()}

    def copy_of(cls, slot, direction, piece):
        layer, kind, part = piece
        who = member_of(kind, layer)
        return pltpu.make_async_remote_copy(
            src_ref=piece_ref(who, part, own=(layer, kind) == (OWN[cls], "c")),
            dst_ref=piece_ref(who, part),
            send_sem=send_sem.at[slot],
            recv_sem=recv_sem.at[who, part],
            device_id=(peers[direction], t),
            device_id_type=MESH,
        )

    def arrive(cls, piece):
        layer, kind, part = piece
        if (layer, kind) == (OWN[cls], "c") or piece in seen[cls]:
            return
        seen[cls].add(piece)
        who = member_of(kind, layer)
        ref = piece_ref(who, part)
        pltpu.make_async_copy(ref, ref, recv_sem.at[who, part]).wait()

    def send(cls, direction, piece):
        arrive(cls, piece)
        copy_of(cls, len(counts[cls]), direction, piece).start()
        counts[cls].append((direction, piece))

    halves = p_send.shape[1]
    ft = ftotal // halves
    rt_rows = tile_of(ft, 16, 448)
    order = {"E": ORDER_E, "M": ORDER_M}
    jobs = [("start",), ("right",)]
    for name in JOBS(len(spans)):
        if name[0] == "main":
            jobs += [name + (h,) for h in range(halves)]
        else:
            jobs.append(name)
    gft = tile_of(ftotal, 16, GRAD_ROWS)
    gtile = tile_of(width, 128, GRAD_COLS)

    def needs_of(cls, job):
        if job[0] == "main":
            layer = order[cls][job[1]]
            return [(layer, kind, p) for kind in "cxyd" for p in (0, *job[2])]
        if job[0] == "weigh":
            return [(layer, kind, 0) for layer in range(4) for kind in "cxyd"]
        return []

    def took(job):
        if job[0] == "main":
            return 0.2 + 3.1 / halves * sum(spans[p - 1][1] for p in job[2]) / width
        return {"start": 0.2, "right": 2.5, "weigh": 0.6, "grad": 1.4}[job[0]]

    slots = {cls: [(needs_of(cls, job), took(job), RIGHT_AT if job[0] == "right" else 0.0) for job in jobs] for cls in "EM"}
    sizes = [facts * width * 2] + [rows * size * 2 for _, size in spans]
    log = plan_links(sizes)
    todo = {cls: plan_core(cls, log, slots) for cls in "EM"}

    local = [
        pltpu.make_async_copy(right_in, rall.at[t], local_sem.at[0]),
        pltpu.make_async_copy(tok_in, tok.at[m].at[:, pl.ds(0, width)], local_sem.at[1]),
        pltpu.make_async_copy(left_in, left.at[m], local_sem.at[2]),
        pltpu.make_async_copy(fit_in, fit, local_sem.at[3]),
        pltpu.make_async_copy(w_in, w.at[pl.ds(low, ftotal), pl.ds(0, width)], local_sem.at[4]),
    ]
    r_copy = pltpu.make_async_remote_copy(
        src_ref=right_in, dst_ref=rall.at[t], send_sem=r_send, recv_sem=r_recv,
        device_id=(m, 1 - t), device_id_type=MESH,
    )

    def do_right():
        kk = lax.broadcasted_iota(jnp.int32, (2 * rall.shape[1], 16 * pad), 0)
        qq = lax.broadcasted_iota(jnp.int32, (2 * rall.shape[1], 16 * pad), 1)
        slot_q = qq % pad
        spread = jnp.where((slot_q < facts) & (kk == facts * (qq // pad) + slot_q), 1.0, 0.0)
        spread = spread.astype(jnp.bfloat16)
        local[0].wait()
        r_copy.wait()
        r_val = jnp.concatenate([rall[0], rall[1]], axis=0)
        rt[...] = lax.dot_general(
            r_val, spread, TN, preferred_element_type=jnp.float32
        ).astype(jnp.bfloat16)

    def padded(value):
        if facts < pad:
            value = jnp.concatenate([value, jnp.zeros((pad - facts, width), value.dtype)], axis=0)
        return value

    def do_weigh():
        slot_row = lax.broadcasted_iota(jnp.int32, (pad, 1), 0) // RANK
        for b in range(16):
            col = jnp.zeros((pad, 1), jnp.float32)
            for r in range(facts // RANK):
                col = jnp.where(slot_row == r, fit[b * (facts // RANK) + r], col)
            wl[pl.ds(b * pad, pad), :] = (padded(left[b]).astype(jnp.float32) * col).astype(jnp.bfloat16)

    def do_grad(i):
        @pl.loop(0, width // gtile)
        def _(j):
            dspan = pl.ds(pl.multiple_of(j * gtile, 128), gtile)
            g = jnp.dot(rt[i * gft:(i + 1) * gft, :], wl[:, dspan], preferred_element_type=jnp.float32)
            grad_ref[i * gft:(i + 1) * gft, dspan] = (g * scale).astype(jnp.bfloat16)

    def exchange(side, piece):
        span = pl.ds(piece * (ftotal // halves), ftotal // halves)
        return pltpu.make_async_remote_copy(
            src_ref=own_ref.at[2 + side].at[span], dst_ref=got_ref.at[side].at[span],
            send_sem=p_send.at[side, piece], recv_sem=p_recv.at[side, piece],
            device_id=(m, 1 - t), device_id_type=MESH,
        )

    group = 4 * rows

    def do_main(step, parts, half):
        l = real(jnp.where(where_am_i["E"], order["E"][step], order["M"][step]))
        side = l % 2
        mine_here = l // 2 == t
        first, last = parts[0] == 1, parts[-1] == len(spans)
        begin, end = spans[parts[0] - 1][0], sum(spans[parts[-1] - 1])
        layer = pl.ds(4 * l, 4)
        inner = low // 2
        slot = jnp.where(mine_here, side, 2 + side)
        if first and half == 0:
            here = inner * (l % 2)
            w[pl.ds(pl.multiple_of(inner - here, 16), inner), :width] = jnp.zeros((inner, width), w.dtype)
            for i in range(4):
                w[pl.ds(pl.multiple_of(here + i * pad, 16), pad), :width] = padded(left[4 * l + i])
            pair = jnp.where(l // 2 == 0, rt[:, :low], rt[:, low:])
            w[low:, width:width + low] = pair
            w[low:, width + low:] = pair

        def dot(row, count, start, stop):
            return lax.dot_general(
                w[row:row + count, start:stop], tok[layer, :, start:stop].reshape(group, stop - start), NT,
                preferred_element_type=jnp.float32,
            )

        def tile(row, count, start, stop):
            value = lax.dot_general(
                w[pl.ds(row, count), start:stop], tok[layer, :, start:stop].reshape(group, stop - start), NT,
                preferred_element_type=jnp.float32,
            )
            return value if first else acc[pl.ds(row, count), :] + value

        if half == 0:
            value = tile(0, low + rt_rows, begin, end)
            if not last:
                acc[:low + rt_rows, :] = value
            else:
                qc = lax.broadcasted_iota(jnp.int32, (low, group), 0)
                rr = lax.broadcasted_iota(jnp.int32, (low, group), 1)
                sq = qc % pad
                mine = (qc // inner == l % 2) & (sq < facts) & (
                    (facts // RANK) * ((qc % inner) // pad) + sq // RANK == rr // MEMBER_TOKENS
                )
                proj = jnp.where(mine, value[:low], 0.0).astype(jnp.bfloat16).astype(jnp.float32)
                proj = mixing * proj.T
                high = proj.astype(jnp.bfloat16)
                rest = (proj - high.astype(jnp.float32)).astype(jnp.bfloat16)
                tok[layer, :, width:width + low] = high.reshape(4, rows, low)
                tok[layer, :, width + low:] = rest.reshape(4, rows, low)
                value = value[low:] + lax.dot_general(
                    w[low:low + rt_rows, width:], tok[layer, :, width:].reshape(group, 2 * low), NT,
                    preferred_element_type=jnp.float32,
                )
                own_ref[slot, :rt_rows, :group] = value.astype(jnp.bfloat16)

        per = ft // rt_rows

        @pl.loop(half * per + (half == 0), (half + 1) * per)
        def _(i):
            row = pl.multiple_of(i * rt_rows, 16)
            value = tile(pl.multiple_of(row + low, 16), rt_rows, begin, width + 2 * low if last else end)
            if last:
                own_ref[slot, pl.ds(row, rt_rows), :group] = value.astype(jnp.bfloat16)
            else:
                acc[pl.ds(pl.multiple_of(row + low, 16), rt_rows), :] = value

        if not last:
            return

        @pl.when(jnp.logical_not(mine_here))
        def _():
            exchange(side, half).start()

    def comm(n):
        for cls in "EM":
            sends, needs = todo[cls][n]
            if n > 0 and not sends and all(need in seen[cls] for need in needs):
                continue

            @pl.when(where_am_i[cls])
            def _(cls=cls, sends=sends, needs=needs):
                for direction, piece in sends:
                    send(cls, direction, piece)
                for need in needs:
                    arrive(cls, need)

    for n, job in enumerate(jobs):
        if n > 1:
            pl.semaphore_wait(step_sem, 1)
        comm(n)
        if 0 < n:
            pl.semaphore_signal(step_sem, inc=1, device_id=(m, 1 - t), device_id_type=MESH)
        if n == 2:
            for copy in local[1:]:
                copy.wait()
        if job[0] == "start":
            r_copy.start()
            for copy in local:
                copy.start()
        elif job[0] == "right":
            do_right()
        elif not COMPUTE:
            pass
        elif job[0] == "weigh":
            do_weigh()
        elif job[0] == "grad":
            do_grad(job[1])
        else:
            do_main(*job[1:])
    pl.semaphore_wait(step_sem, 1)
    comm(len(jobs))

    for cls in "EM":
        @pl.when(where_am_i[cls])
        def _(cls=cls):
            for layer in range(4):
                for kind in "cxyd":
                    for part in range(len(spans) + 1):
                        arrive(cls, (layer, kind, part))
            for slot, (direction, piece) in enumerate(counts[cls]):
                copy_of(cls, slot, direction, piece).wait_send()
    if COMPUTE:
        for side in range(2):
            for piece in range(halves):
                exchange(side, piece).wait()


def finish_kernel(grad, own, got, h_ref, g_ref, hv, g_sem, h_sem):
    columns = own.shape[1]
    n = hv.shape[1] // 2
    gp, hp = g_sem.shape[0], h_sem.shape[0]

    def copy(src, dst, sem, pieces, i):
        span = pl.ds(i * (columns // pieces), columns // pieces)
        return pltpu.make_async_copy(src.at[span], dst.at[span], sem.at[i])

    for i in range(gp):
        copy(grad, g_ref, g_sem, gp, i).start()
    for i in range(hp):
        span = pl.ds(i * (columns // hp), columns // hp)
        for side in range(2):
            total = own[side, span, :n].astype(jnp.float32) + got[side, span, :n].astype(jnp.float32)
            hv[span, side * n:(side + 1) * n] = total.astype(jnp.bfloat16)
        copy(hv, h_ref, h_sem, hp, i).start()
    for i in range(gp):
        copy(grad, g_ref, g_sem, gp, i).wait()
    for i in range(hp):
        copy(hv, h_ref, h_sem, hp, i).wait()


def body(tokens, up_weight, left_factors, right_factors, fitness):
    noise_scale = 0.25 * D ** (-0.5)
    mixing = noise_scale * RANK ** (-0.5)
    rows, width = tokens.shape
    facts = left_factors.shape[0]
    columns = up_weight.shape[1]
    rrows = right_factors.shape[0]
    pad = -(-facts // 16) * 16
    members = fitness.shape[0]
    bf, f32 = jnp.bfloat16, jnp.float32
    hbm = pl.BlockSpec(memory_space=pltpu.HBM)
    vm = pl.BlockSpec(memory_space=pltpu.VMEM)
    dma = pltpu.SemaphoreType.DMA
    edges = [width * n // 10 // 128 * 128 for n in CUTS]
    spans = [(a, b - a) for a, b in zip(edges, edges[1:])]
    halves = 2 if columns % 32 == 0 else 1
    lanes = -(-4 * rows // 128) * 128
    scale = 1.0 / (members * noise_scale * RANK**0.5)
    grad, own, got = pl.pallas_call(
        functools.partial(gather_kernel, mixing, scale, spans),
        out_shape=(
            jax.ShapeDtypeStruct((columns, width), bf),
            jax.ShapeDtypeStruct((4, columns, lanes), bf),
            jax.ShapeDtypeStruct((2, columns, lanes), bf),
        ),
        in_specs=[hbm] * 5,
        out_specs=(vm, vm, vm),
        scratch_shapes=[
            pltpu.VMEM((16, rows, width + 16 * pad), bf),
            pltpu.VMEM((16, facts, width), bf),
            pltpu.VMEM((8 * pad + columns, width + 16 * pad), bf),
            pltpu.VMEM((2, rrows, columns), bf),
            pltpu.VMEM((8 * pad + columns, 4 * rows), f32),
            pltpu.VMEM((columns, 16 * pad), bf),
            pltpu.VMEM((16 * pad, width), bf),
            pltpu.SMEM((members,), f32),
            dma((40 * (1 + len(spans)),)), dma((16, 1 + len(spans))), dma((5,)), dma, dma, dma((2, halves)), dma((2, halves)), pltpu.SemaphoreType.REGULAR,
        ],
        compiler_params=pltpu.CompilerParams(
            collective_id=0, has_side_effects=True, vmem_limit_bytes=28 * 1024 * 1024
        ),
        name="gather_project",
    )(
        pltpu.with_memory_space_constraint(tokens, pltpu.HBM),
        pltpu.with_memory_space_constraint(up_weight.T, pltpu.HBM),
        pltpu.with_memory_space_constraint(left_factors, pltpu.HBM),
        pltpu.with_memory_space_constraint(right_factors, pltpu.HBM),
        pltpu.with_memory_space_constraint(fitness, pltpu.HBM),
    )
    pieces = 4 if columns % 64 == 0 else 1
    hidden, gradient = pl.pallas_call(
        finish_kernel,
        out_shape=(
            jax.ShapeDtypeStruct((columns, 8 * rows), bf),
            jax.ShapeDtypeStruct((columns, width), bf),
        ),
        in_specs=[vm, vm, vm],
        out_specs=(hbm, hbm),
        scratch_shapes=[pltpu.VMEM((columns, 8 * rows), bf), dma((pieces,)), dma((pieces,))],
        compiler_params=pltpu.CompilerParams(vmem_limit_bytes=8 * 1024 * 1024),
        name="finish",
    )(grad, own, got)
    return hidden.T, gradient.T


def solution(mesh):
    fits = mesh.shape["member"] == 16 and mesh.shape["tensor"] == 2
    return jax.shard_map(
        body if fits else plain_body,
        mesh=mesh,
        in_specs=(
            P("member", "tensor"),
            P("tensor", "member"),
            P("member", "tensor"),
            P("tensor", "member"),
            P(),
        ),
        out_specs=(P("tensor", "member"), P("tensor", "member")),
        check_vma=False,
    )
```

```python
import functools

import jax
import jax.numpy as jnp
from jax import lax
from jax.experimental import pallas as pl
from jax.experimental.pallas import tpu as pltpu
from jax.sharding import PartitionSpec as P

D = 5120
RANK = 4
MEMBER_TOKENS = 16
MESH = pl.DeviceIdType.MESH
NT = (((1,), (1,)), ((), ()))
TN = (((0,), (0,)), ((), ()))


def plain_body(tokens, up_weight, left_factors, right_factors, fitness):
    noise_scale = 0.25 * D ** (-0.5)
    mixing = noise_scale * RANK ** (-0.5)
    width = tokens.shape[1]
    columns = up_weight.shape[1]
    right_all = lax.all_gather(right_factors, "tensor", axis=0, tiled=True)
    members = right_all.shape[0] // RANK
    left_all = lax.all_gather(left_factors, "member", axis=0, tiled=True)
    all_tokens = lax.all_gather(tokens, "member", axis=0, tiled=True)
    projection = jnp.einsum(
        "uzg,uig->uzi",
        all_tokens.reshape(members, MEMBER_TOKENS, width),
        left_all.reshape(members, RANK, width),
        preferred_element_type=jnp.float32,
    ).astype(jnp.bfloat16)
    base = jnp.dot(all_tokens, up_weight, preferred_element_type=jnp.float32)
    correction = jnp.einsum(
        "djt,dty->djy",
        projection,
        right_all.reshape(members, RANK, columns),
        preferred_element_type=jnp.float32,
    ).reshape(base.shape)
    summed = lax.psum_scatter(
        (base + mixing * correction).astype(jnp.bfloat16), "tensor", scatter_dimension=0, tiled=True
    )
    fit_rows = jnp.repeat(fitness, RANK)
    weighted = (fit_rows[:, None] * left_all.astype(jnp.float32)).astype(jnp.bfloat16)
    gradient = jnp.einsum("kd,kf->df", weighted, right_all, preferred_element_type=jnp.float32)
    gradient = gradient * (1.0 / (members * noise_scale * RANK**0.5))
    return (summed, gradient.astype(jnp.bfloat16))


ACROSS_X = {"c": "x", "x": "c", "y": "d", "d": "y"}
ACROSS_Y = {"c": "y", "y": "c", "x": "d", "d": "x"}
LINKS = {
    "Ex": ("E", "E", "x"), "Ey": ("E", "E", "y"), "Eu": ("E", "M", "u"), "Mv": ("M", "E", "v"),
    "Mu": ("M", "M", "u"), "Mx": ("M", "M", "x"), "My": ("M", "M", "y"),
}
OWN = {"E": 0, "M": 1}
BASE = {
    "Ex": {"x": -0.4, "d": 2.7},
    "Ey": {"y": 4.4, "d": 0.4},
    "Eu": {"c": 1.1, "x": 5.0, "y": 2.5, "d": 3.0},
    "Mv": {"c": 2.4, "d": 5.1},
    "Mu": {"c": -1.3, "x": 5.3, "y": 13.1, "d": -0.8},
    "Mx": {"x": 0.0, "d": 3.8},
    "My": {"y": -1.4, "d": -0.5},
}
RANKS = {"E": (-6.9, 0.7, 2.6, 3.9), "M": (1.8, -6.3, 5.0, 6.2)}
LAYER_WEIGHT, PART_WEIGHT, LEFT_FIRST = 1.0, 0.12, 7.7
CUTS = (0, 5, 10)
ORDER_E, ORDER_M = (0, 1, 2, 3), (1, 0, 2, 3)
LEAD = 2.0
COMPUTE = True


def JOBS(parts):
    every = tuple(range(1, parts + 1))
    early = [[("main", g, every)] for g in range(3)]
    late = [("main", 3, every[:-1]), ("main", 3, every[-1:])]
    return early[0] + [("weigh",)] + [("grad", j) for j in range(4)] + early[1] + [("main", 2, every[:-1]), ("main", 2, every[-1:])] + late


RIGHT_AT = 2.5
GRAD_ROWS, GRAD_COLS = 432, 1280
BYTES_PER_US = 85e3 / 2
HOP_US = 2.0


def landed_as(link, layer, kind):
    if link[1] == "x":
        return layer, ACROSS_X[kind]
    if link[1] == "y":
        return layer, ACROSS_Y[kind]
    return (3 - layer if link == "Mu" else layer), kind


def plan_links(sizes):
    parts = range(len(sizes))
    have = {c: {(OWN[c], "c", p): 0.0 for p in parts} for c in OWN}
    claimed = {c: set(have[c]) for c in OWN}
    free = {link: 0.0 for link in LINKS}
    log, times = [], {0.0}
    while any(len(claimed[c]) < 16 * len(sizes) for c in OWN):
        now = min(times)
        times = {t for t in times if t > now + 1e-6}
        for link, (src, dst, _) in LINKS.items():
            if free[link] > now + 1e-6:
                continue
            choices = []
            for (layer, kind, p), at in have[src].items():
                there = landed_as(link, layer, kind) + (p,)
                base = BASE[link].get(there[1])
                if at > now + 1e-6 or there in claimed[dst] or base is None:
                    continue
                score = base + LAYER_WEIGHT * RANKS[dst][there[0]] + PART_WEIGHT * p - (LEFT_FIRST if p == 0 else 0)
                choices.append((round(score, 6), len(choices), (layer, kind, p), there))
            if choices:
                _, _, here, there = min(choices)
                free[link] = now + sizes[here[2]] / BYTES_PER_US
                lands = free[link] + HOP_US
                claimed[dst].add(there)
                have[dst][there] = lands
                log.append((now, link, here, there, lands))
                times |= {free[link], lands}
    return log


def plan_core(cls, log, slots, lead=LEAD):
    lands = {there: at for _, link, _, there, at in log if LINKS[link][1] == cls}
    lands.update({(OWN[cls], "c", p): 0.0 for p in range(16)})
    sends = sorted(
        (max(lands[here], start - lead), n, link, here)
        for n, (start, link, here, _, _) in enumerate(log) if LINKS[link][0] == cls
    )
    now, before, todo = 0.0, [], []
    for needs, took, _ in slots[cls]:
        ready = max([lands[need] for need in needs], default=0.0)
        while sends and sends[0][0] <= max(now, ready):
            at, _, link, here = sends.pop(0)
            now = max(now, at) + 0.05
            todo.append((LINKS[link][2], here))
        now = max(now, ready) + took
        before.append((todo, needs))
        todo = []
    before.append((todo + [(LINKS[s[2]][2], s[3]) for s in sends], []))
    return before


def tile_of(n, step, most):
    best = step
    for size in range(step, most + 1, step):
        if n % size == 0:
            best = size
    return best


def gather_kernel(
    mixing, scale, spans,
    tok_in, w_in, left_in, right_in, fit_in,
    grad_ref, own_ref, got_ref,
    tok, left, w, rall, acc, rt, wl, fit,
    send_sem, recv_sem, local_sem, r_send, r_recv, p_send, p_recv, step_sem,
):
    m = lax.axis_index("member")
    t = lax.axis_index("tensor")
    z, y, x = m // 4, (m // 2) % 2, m % 2
    rows, width = tok_in.shape
    facts = left_in.shape[0]
    pad = wl.shape[0] // 16
    ftotal = w_in.shape[0]
    low = w.shape[0] - ftotal
    far = z >= 2
    toward = jnp.where(far, -1, 1)
    where_am_i = {"E": (z == 0) | (z == 3), "M": (z == 1) | (z == 2)}

    def at(l, yy, xx):
        return 4 * l + 2 * yy + xx

    def real(layer):
        return jnp.where(far, 3 - layer, layer)

    def member_of(kind, layer):
        return at(real(layer), 1 - y if kind in "yd" else y, 1 - x if kind in "xd" else x)

    peers = {"x": at(z, y, 1 - x), "y": at(z, 1 - y, x), "u": m + 4 * toward, "v": m - 4 * toward}
    hops = {"E": "xyu", "M": "xyuv"}

    barrier = pltpu.get_barrier_semaphore()
    pl.semaphore_signal(barrier, inc=1, device_id=(m, 1 - t), device_id_type=MESH)
    for cls in "EM":
        @pl.when(where_am_i[cls])
        def _(cls=cls):
            for d in hops[cls]:
                pl.semaphore_signal(barrier, inc=1, device_id=(peers[d], t), device_id_type=MESH)
            pl.semaphore_wait(barrier, 1 + len(hops[cls]))

    def piece_ref(who, part, own=False):
        if part == 0:
            return left_in if own else left.at[who]
        start, size = spans[part - 1]
        return (tok_in if own else tok.at[who]).at[:, pl.ds(start, size)]

    counts = {"E": [], "M": []}
    seen = {"E": set(), "M": set()}

    def copy_of(cls, slot, direction, piece):
        layer, kind, part = piece
        who = member_of(kind, layer)
        return pltpu.make_async_remote_copy(
            src_ref=piece_ref(who, part, own=(layer, kind) == (OWN[cls], "c")),
            dst_ref=piece_ref(who, part),
            send_sem=send_sem.at[slot],
            recv_sem=recv_sem.at[who, part],
            device_id=(peers[direction], t),
            device_id_type=MESH,
        )

    def arrive(cls, piece):
        layer, kind, part = piece
        if (layer, kind) == (OWN[cls], "c") or piece in seen[cls]:
            return
        seen[cls].add(piece)
        who = member_of(kind, layer)
        ref = piece_ref(who, part)
        pltpu.make_async_copy(ref, ref, recv_sem.at[who, part]).wait()

    def send(cls, direction, piece):
        arrive(cls, piece)
        copy_of(cls, len(counts[cls]), direction, piece).start()
        counts[cls].append((direction, piece))

    halves = p_send.shape[1]
    ft = ftotal // halves
    rt_rows = tile_of(ft, 16, 448)
    order = {"E": ORDER_E, "M": ORDER_M}
    jobs = [("start",), ("right",)]
    for name in JOBS(len(spans)):
        if name[0] == "main":
            jobs += [name + (h,) for h in range(halves)]
        else:
            jobs.append(name)
    gft = tile_of(ftotal, 16, GRAD_ROWS)
    gtile = tile_of(width, 128, GRAD_COLS)

    def needs_of(cls, job):
        if job[0] == "main":
            layer = order[cls][job[1]]
            return [(layer, kind, p) for kind in "cxyd" for p in (0, *job[2])]
        if job[0] == "weigh":
            return [(layer, kind, 0) for layer in range(4) for kind in "cxyd"]
        return []

    def took(job):
        if job[0] == "main":
            return 0.2 + 3.1 / halves * sum(spans[p - 1][1] for p in job[2]) / width
        return {"start": 0.2, "right": 2.5, "weigh": 0.6, "grad": 1.4}[job[0]]

    slots = {cls: [(needs_of(cls, job), took(job), RIGHT_AT if job[0] == "right" else 0.0) for job in jobs] for cls in "EM"}
    sizes = [facts * width * 2] + [rows * size * 2 for _, size in spans]
    log = plan_links(sizes)
    todo = {cls: plan_core(cls, log, slots) for cls in "EM"}

    local = [
        pltpu.make_async_copy(right_in, rall.at[t], local_sem.at[0]),
        pltpu.make_async_copy(tok_in, tok.at[m].at[:, pl.ds(0, width)], local_sem.at[1]),
        pltpu.make_async_copy(left_in, left.at[m], local_sem.at[2]),
        pltpu.make_async_copy(fit_in, fit, local_sem.at[3]),
        pltpu.make_async_copy(w_in, w.at[pl.ds(low, ftotal), pl.ds(0, width)], local_sem.at[4]),
    ]
    r_copy = pltpu.make_async_remote_copy(
        src_ref=right_in, dst_ref=rall.at[t], send_sem=r_send, recv_sem=r_recv,
        device_id=(m, 1 - t), device_id_type=MESH,
    )

    def do_right():
        kk = lax.broadcasted_iota(jnp.int32, (2 * rall.shape[1], 16 * pad), 0)
        qq = lax.broadcasted_iota(jnp.int32, (2 * rall.shape[1], 16 * pad), 1)
        slot_q = qq % pad
        spread = jnp.where((slot_q < facts) & (kk == facts * (qq // pad) + slot_q), 1.0, 0.0)
        spread = spread.astype(jnp.bfloat16)
        local[0].wait()
        r_copy.wait()
        r_val = jnp.concatenate([rall[0], rall[1]], axis=0)
        rt[...] = lax.dot_general(
            r_val, spread, TN, preferred_element_type=jnp.float32
        ).astype(jnp.bfloat16)

    def padded(value):
        if facts < pad:
            value = jnp.concatenate([value, jnp.zeros((pad - facts, width), value.dtype)], axis=0)
        return value

    def do_weigh():
        slot_row = lax.broadcasted_iota(jnp.int32, (pad, 1), 0) // RANK
        for b in range(16):
            col = jnp.zeros((pad, 1), jnp.float32)
            for r in range(facts // RANK):
                col = jnp.where(slot_row == r, fit[b * (facts // RANK) + r], col)
            wl[pl.ds(b * pad, pad), :] = (padded(left[b]).astype(jnp.float32) * col).astype(jnp.bfloat16)

    def do_grad(i):
        @pl.loop(0, width // gtile)
        def _(j):
            dspan = pl.ds(pl.multiple_of(j * gtile, 128), gtile)
            g = jnp.dot(rt[i * gft:(i + 1) * gft, :], wl[:, dspan], preferred_element_type=jnp.float32)
            grad_ref[i * gft:(i + 1) * gft, dspan] = (g * scale).astype(jnp.bfloat16)

    def exchange(side, piece):
        span = pl.ds(piece * (ftotal // halves), ftotal // halves)
        return pltpu.make_async_remote_copy(
            src_ref=own_ref.at[2 + side].at[span], dst_ref=got_ref.at[side].at[span],
            send_sem=p_send.at[side, piece], recv_sem=p_recv.at[side, piece],
            device_id=(m, 1 - t), device_id_type=MESH,
        )

    group = 4 * rows

    def do_main(step, parts, half):
        l = real(jnp.where(where_am_i["E"], order["E"][step], order["M"][step]))
        side = l % 2
        mine_here = l // 2 == t
        first, last = parts[0] == 1, parts[-1] == len(spans)
        begin, end = spans[parts[0] - 1][0], sum(spans[parts[-1] - 1])
        layer = pl.ds(4 * l, 4)
        inner = low // 2
        slot = jnp.where(mine_here, side, 2 + side)
        if first and half == 0:
            here = inner * (l % 2)
            w[pl.ds(pl.multiple_of(inner - here, 16), inner), :width] = jnp.zeros((inner, width), w.dtype)
            for i in range(4):
                w[pl.ds(pl.multiple_of(here + i * pad, 16), pad), :width] = padded(left[4 * l + i])
            pair = jnp.where(l // 2 == 0, rt[:, :low], rt[:, low:])
            w[low:, width:width + low] = pair
            w[low:, width + low:] = pair

        def dot(row, count, start, stop):
            return lax.dot_general(
                w[row:row + count, start:stop], tok[layer, :, start:stop].reshape(group, stop - start), NT,
                preferred_element_type=jnp.float32,
            )

        def tile(row, count, start, stop):
            value = lax.dot_general(
                w[pl.ds(row, count), start:stop], tok[layer, :, start:stop].reshape(group, stop - start), NT,
                preferred_element_type=jnp.float32,
            )
            return value if first else acc[pl.ds(row, count), :] + value

        if half == 0:
            value = tile(0, low + rt_rows, begin, end)
            if not last:
                acc[:low + rt_rows, :] = value
            else:
                qc = lax.broadcasted_iota(jnp.int32, (low, group), 0)
                rr = lax.broadcasted_iota(jnp.int32, (low, group), 1)
                sq = qc % pad
                mine = (qc // inner == l % 2) & (sq < facts) & (
                    (facts // RANK) * ((qc % inner) // pad) + sq // RANK == rr // MEMBER_TOKENS
                )
                proj = jnp.where(mine, value[:low], 0.0).astype(jnp.bfloat16).astype(jnp.float32)
                proj = mixing * proj.T
                high = proj.astype(jnp.bfloat16)
                rest = (proj - high.astype(jnp.float32)).astype(jnp.bfloat16)
                tok[layer, :, width:width + low] = high.reshape(4, rows, low)
                tok[layer, :, width + low:] = rest.reshape(4, rows, low)
                value = value[low:] + lax.dot_general(
                    w[low:low + rt_rows, width:], tok[layer, :, width:].reshape(group, 2 * low), NT,
                    preferred_element_type=jnp.float32,
                )
                own_ref[slot, :rt_rows, :group] = value.astype(jnp.bfloat16)

        per = ft // rt_rows

        @pl.loop(half * per + (half == 0), (half + 1) * per)
        def _(i):
            row = pl.multiple_of(i * rt_rows, 16)
            value = tile(pl.multiple_of(row + low, 16), rt_rows, begin, width + 2 * low if last else end)
            if last:
                own_ref[slot, pl.ds(row, rt_rows), :group] = value.astype(jnp.bfloat16)
            else:
                acc[pl.ds(pl.multiple_of(row + low, 16), rt_rows), :] = value

        if not last:
            return

        @pl.when(jnp.logical_not(mine_here))
        def _():
            exchange(side, half).start()

    def comm(n):
        for cls in "EM":
            sends, needs = todo[cls][n]
            if n > 0 and not sends and all(need in seen[cls] for need in needs):
                continue

            @pl.when(where_am_i[cls])
            def _(cls=cls, sends=sends, needs=needs):
                for direction, piece in sends:
                    send(cls, direction, piece)
                for need in needs:
                    arrive(cls, need)

    for n, job in enumerate(jobs):
        if n > 1:
            @pl.when(t == 1)
            def _():
                pl.semaphore_wait(step_sem, 1)
        comm(n)
        if 0 < n:
            @pl.when(t == 0)
            def _():
                pl.semaphore_signal(step_sem, inc=1, device_id=(m, 1 - t), device_id_type=MESH)
        if n == 2:
            for copy in local[1:]:
                copy.wait()
        if job[0] == "start":
            r_copy.start()
            for copy in local:
                copy.start()
        elif job[0] == "right":
            do_right()
        elif not COMPUTE:
            pass
        elif job[0] == "weigh":
            do_weigh()
        elif job[0] == "grad":
            do_grad(job[1])
        else:
            do_main(*job[1:])

    @pl.when(t == 1)
    def _():
        pl.semaphore_wait(step_sem, 1)

    comm(len(jobs))

    for cls in "EM":
        @pl.when(where_am_i[cls])
        def _(cls=cls):
            for layer in range(4):
                for kind in "cxyd":
                    for part in range(len(spans) + 1):
                        arrive(cls, (layer, kind, part))
            for slot, (direction, piece) in enumerate(counts[cls]):
                copy_of(cls, slot, direction, piece).wait_send()
    if COMPUTE:
        for side in range(2):
            for piece in range(halves):
                exchange(side, piece).wait()


def finish_kernel(grad, own, got, h_ref, g_ref, hv, g_sem, h_sem):
    columns = own.shape[1]
    n = hv.shape[1] // 2
    gp, hp = g_sem.shape[0], h_sem.shape[0]

    def copy(src, dst, sem, pieces, i):
        span = pl.ds(i * (columns // pieces), columns // pieces)
        return pltpu.make_async_copy(src.at[span], dst.at[span], sem.at[i])

    for i in range(gp):
        copy(grad, g_ref, g_sem, gp, i).start()
    for i in range(hp):
        span = pl.ds(i * (columns // hp), columns // hp)
        for side in range(2):
            total = own[side, span, :n].astype(jnp.float32) + got[side, span, :n].astype(jnp.float32)
            hv[span, side * n:(side + 1) * n] = total.astype(jnp.bfloat16)
        copy(hv, h_ref, h_sem, hp, i).start()
    for i in range(gp):
        copy(grad, g_ref, g_sem, gp, i).wait()
    for i in range(hp):
        copy(hv, h_ref, h_sem, hp, i).wait()


def body(tokens, up_weight, left_factors, right_factors, fitness):
    noise_scale = 0.25 * D ** (-0.5)
    mixing = noise_scale * RANK ** (-0.5)
    rows, width = tokens.shape
    facts = left_factors.shape[0]
    columns = up_weight.shape[1]
    rrows = right_factors.shape[0]
    pad = -(-facts // 16) * 16
    members = fitness.shape[0]
    bf, f32 = jnp.bfloat16, jnp.float32
    hbm = pl.BlockSpec(memory_space=pltpu.HBM)
    vm = pl.BlockSpec(memory_space=pltpu.VMEM)
    dma = pltpu.SemaphoreType.DMA
    edges = [width * n // 10 // 128 * 128 for n in CUTS]
    spans = [(a, b - a) for a, b in zip(edges, edges[1:])]
    halves = 2 if columns % 32 == 0 else 1
    lanes = -(-4 * rows // 128) * 128
    scale = 1.0 / (members * noise_scale * RANK**0.5)
    grad, own, got = pl.pallas_call(
        functools.partial(gather_kernel, mixing, scale, spans),
        out_shape=(
            jax.ShapeDtypeStruct((columns, width), bf),
            jax.ShapeDtypeStruct((4, columns, lanes), bf),
            jax.ShapeDtypeStruct((2, columns, lanes), bf),
        ),
        in_specs=[hbm] * 5,
        out_specs=(vm, vm, vm),
        scratch_shapes=[
            pltpu.VMEM((16, rows, width + 16 * pad), bf),
            pltpu.VMEM((16, facts, width), bf),
            pltpu.VMEM((8 * pad + columns, width + 16 * pad), bf),
            pltpu.VMEM((2, rrows, columns), bf),
            pltpu.VMEM((8 * pad + columns, 4 * rows), f32),
            pltpu.VMEM((columns, 16 * pad), bf),
            pltpu.VMEM((16 * pad, width), bf),
            pltpu.SMEM((members,), f32),
            dma((40 * (1 + len(spans)),)), dma((16, 1 + len(spans))), dma((5,)), dma, dma, dma((2, halves)), dma((2, halves)), pltpu.SemaphoreType.REGULAR,
        ],
        compiler_params=pltpu.CompilerParams(
            collective_id=0, has_side_effects=True, vmem_limit_bytes=28 * 1024 * 1024
        ),
        name="gather_project",
    )(
        pltpu.with_memory_space_constraint(tokens, pltpu.HBM),
        pltpu.with_memory_space_constraint(up_weight.T, pltpu.HBM),
        pltpu.with_memory_space_constraint(left_factors, pltpu.HBM),
        pltpu.with_memory_space_constraint(right_factors, pltpu.HBM),
        pltpu.with_memory_space_constraint(fitness, pltpu.HBM),
    )
    pieces = 4 if columns % 64 == 0 else 1
    hidden, gradient = pl.pallas_call(
        finish_kernel,
        out_shape=(
            jax.ShapeDtypeStruct((columns, 8 * rows), bf),
            jax.ShapeDtypeStruct((columns, width), bf),
        ),
        in_specs=[vm, vm, vm],
        out_specs=(hbm, hbm),
        scratch_shapes=[pltpu.VMEM((columns, 8 * rows), bf), dma((pieces,)), dma((pieces,))],
        compiler_params=pltpu.CompilerParams(vmem_limit_bytes=8 * 1024 * 1024),
        name="finish",
    )(grad, own, got)
    return hidden.T, gradient.T


def solution(mesh):
    fits = mesh.shape["member"] == 16 and mesh.shape["tensor"] == 2
    return jax.shard_map(
        body if fits else plain_body,
        mesh=mesh,
        in_specs=(
            P("member", "tensor"),
            P("tensor", "member"),
            P("member", "tensor"),
            P("tensor", "member"),
            P(),
        ),
        out_specs=(P("tensor", "member"), P("tensor", "member")),
        check_vma=False,
    )
```
